32 devices in a mesh: row: 4 (over y, x), col: 8 (over z, core).
Axes of the slice: x: 2, y: 2, z: 4, core: 2. Of those that a mesh axis runs over, the one named last changes fastest.
Arguments:
- amplitudes: bfloat16 [4096, 262144], P(None, ('row', 'col')), may hold values from -6 to 6
- integrals: bfloat16 [64, 262144], P(None, ('row', 'col')), may hold values from -6 to 6
- hh_coupling: bfloat16 [64, 4096], P('row'), may hold values from -0.09375 to 0.09375
- thc_factor: bfloat16 [512, 1024], P(None, ('row', 'col')), may hold values from -0.25 to 0.25
- thc_core: float32 [1024, 1024], P('col', 'row'), may hold values from -3 to 3
- occ_energy: float32 [64], replicated, may hold values from -2 to -0.5
- vir_energy: float32 [512], replicated, may hold values from 0.3 to 3
- pair_owner: int32 [64], replicated, may hold values from 0 to 4095, as said below
Outputs:
- updated: bfloat16 [64, 262144], P(None, ('row', 'col'))
The draws below stay inside these ranges and needn't reach their ends.
Inputs may be any that keep to these rules, and one draw needn't show every extreme that they name: pair_owner holds 64 distinct occupied pairs.
All inputs are finite; a program needn't handle non-finite values.
Results may differ from the reference program's by a relative error of at most 0.007.
Values may be sent and summed in bfloat16 or wider, within the bound.
No kernel may reach another device: no remote copies, remote signals or barrier semaphores. Data moves between devices by JAX's collectives and lax.ppermute only.
A program may use at most 128 MiB of HBM per device.

```python
import math
import jax
import jax.numpy as jnp
from jax import lax

OCC = 64
VIR = 512
NPTS = 1024
PC = 8
PW = 64
N_ROW = 4
N_COL = 8


def draw_pair_owner(key, part):
    return jax.random.permutation(key, OCC * OCC)[:PW].astype(jnp.int32)


def steps_of(key, dims, cuts, low, high):
    factor_of = 1.0
    for axis_at, shards_of in cuts:
        heights = jax.random.uniform(jax.random.fold_in(jax.random.fold_in(key, 6), axis_at), (shards_of,), jnp.float32, low / len(cuts), high / len(cuts))
        factor_of = factor_of * jnp.repeat(jnp.exp(heights), dims[axis_at] // shards_of).reshape((-1,) + (1,) * (len(dims) - 1 - axis_at))
    return factor_of


def bell_draw(stream_key, dims, deviation, most, split=(), dtype=jnp.bfloat16):
    array = deviation * jax.random.normal(stream_key, dims, jnp.float32)
    if split:
        array = array * steps_of(stream_key, dims, split, -0.22, 0.18)
    return jnp.clip(array, -most, most).astype(dtype)


def setup_inputs(seed: int = 0) -> dict:
    key_list = jax.random.split(jax.random.key(seed), 9)
    return {
        "amplitudes": bell_draw(key_list[0], (OCC * OCC, VIR * VIR), 1.0, 6.0, ((1, 32),)),
        "integrals": bell_draw(key_list[1], (PW, VIR * VIR), 1.0, 6.0, ((1, 32),)),
        "hh_coupling": bell_draw(key_list[2], (PW, OCC * OCC), (OCC * OCC) ** -0.5, 0.09375, ((0, 4),)),
        "thc_factor": bell_draw(key_list[3], (VIR, NPTS), VIR ** -0.5, 0.25, ((1, 32),)),
        "thc_core": bell_draw(key_list[4], (NPTS, NPTS), 0.5, 3.0, ((0, 8), (1, 4)), jnp.float32),
        "occ_energy": jnp.clip(jax.random.uniform(key_list[5], (OCC,), jnp.float32, -2.0, -0.5), -2.0, -0.5),
        "vir_energy": jnp.clip(jnp.exp(jax.random.uniform(key_list[6], (VIR,), jnp.float32, math.log(0.3), math.log(3.0))), 0.3, 3.0),
        "pair_owner": draw_pair_owner(jax.random.fold_in(key_list[8], 71), 0),
    }


def ladder_block(amps_block, thc_factor, thc_core):
    factor = thc_factor.astype(jnp.float32)
    block_points = NPTS // N_ROW
    half = jnp.einsum('pcd,dq->pcq', amps_block.astype(jnp.float32), factor).astype(jnp.bfloat16)
    middle = jnp.einsum('cP,pcq->pPq', factor, half.astype(jnp.float32))
    weighted = (thc_core[None] * middle).astype(jnp.bfloat16)
    back = jnp.einsum('aP,pPq->paq', factor, weighted.astype(jnp.float32)).astype(jnp.bfloat16)
    back_split = back.astype(jnp.float32).reshape(PC, VIR, N_ROW, block_points)
    factor_split = factor.reshape(VIR, N_ROW, block_points)
    partial_value = jnp.einsum('parq,brq->rpab', back_split, factor_split).astype(jnp.bfloat16)
    partial_value = lax.optimization_barrier(partial_value)
    return jnp.sum(partial_value.astype(jnp.float32), axis=0).astype(jnp.bfloat16)


def reference(amplitudes, integrals, hh_coupling, thc_factor, thc_core, occ_energy, vir_energy, pair_owner):
    coupled = jnp.dot(hh_coupling, amplitudes, preferred_element_type=jnp.float32)
    owned = amplitudes[pair_owner]
    blocks = owned.reshape(N_COL, PC, VIR, VIR)
    ladder = lax.map(lambda blk: ladder_block(blk, thc_factor, thc_core), blocks)
    ladder = ladder.reshape(PW, VIR * VIR)
    first_occ = occ_energy[pair_owner // OCC]
    second_occ = occ_energy[pair_owner % OCC]
    vir_pairs = (vir_energy[:, None] + vir_energy[None, :]).reshape(1, VIR * VIR)
    denom = vir_pairs - (first_occ + second_occ)[:, None]
    rest = (integrals.astype(jnp.float32) + coupled) + ladder.astype(jnp.float32)
    update = 0.4 * owned.astype(jnp.float32) + 0.6 * rest / denom
    return update.astype(jnp.bfloat16)
```

```python
import functools
import jax
import jax.numpy as jnp
from jax import lax
from jax.experimental import pallas as pl
from jax.experimental.pallas import tpu as pltpu
from jax.sharding import PartitionSpec as P

F32, BF16 = jnp.float32, jnp.bfloat16
AXES = ("row", "col")


def dot(a, b, ca, cb):
    return lax.dot_general(a, b, (((ca,), (cb,)), ((), ())), preferred_element_type=F32)


def exchange(value, flip_row, flip_col):
    rows, cols = lax.axis_size("row"), lax.axis_size("col")
    pairs = [
        (r * cols + c, (r ^ flip_row) * cols + (c ^ flip_col))
        for r in range(rows)
        for c in range(cols)
    ]
    return lax.ppermute(value, AXES, pairs)


def owner_terms(pair_owner, occ_energy):
    occupied = occ_energy.shape[0]
    orbital_ids = jnp.arange(occupied, dtype=jnp.int32)
    first_hit = (pair_owner // occupied)[:, None] == orbital_ids[None, :]
    second_hit = (pair_owner % occupied)[:, None] == orbital_ids[None, :]
    first_occ = jnp.sum(jnp.where(first_hit, occ_energy[None, :], 0.0), axis=1)
    second_occ = jnp.sum(jnp.where(second_hit, occ_energy[None, :], 0.0), axis=1)
    return first_occ + second_occ


def place_kernel(spec, *refs):
    parts, points, virtual = spec
    n_in = len(parts)
    ins, (xt_ref, x_ref, core_ref) = refs[:n_in], refs[n_in:]
    row, col = lax.axis_index("row"), lax.axis_index("col")
    wide = virtual // 2
    for ref, entries in zip(ins, parts):
        for slot, (flip_row, flip_col) in enumerate(entries):
            r, c = row ^ flip_row, col ^ flip_col
            cols = lax.axis_size("col")
            j = r * cols + c
            fine = points // (lax.axis_size("row") * cols)
            deep = points // cols
            at = pl.multiple_of(j * fine, fine)
            xt_ref[pl.ds(at, fine), :wide] = ref[slot, :fine, :]
            xt_ref[pl.ds(at, fine), wide:] = ref[slot, fine : 2 * fine, :]
            core_ref[r, pl.ds(pl.multiple_of(c * deep, deep), deep), :] = ref[slot, 2 * fine :, :]
    x_ref[...] = xt_ref[...].T


def ladder_kernel(a_ref, xt_ref, x_ref, core_ref, out_ref, acc_ref):
    blocks, points, block = core_ref.shape
    virtual = xt_ref.shape[1]
    a = a_ref[...].reshape(virtual, virtual)
    for r in range(blocks):
        xq = xt_ref[r * block : (r + 1) * block, :]
        half = dot(a, xq, 1, 1).astype(BF16)
        middle = dot(xt_ref[...], half, 1, 0)
        weighted = (core_ref[r].astype(F32) * middle).astype(BF16)
        back = dot(x_ref[...], weighted, 1, 0).astype(BF16)
        term = dot(back, xq, 1, 0)
        if r == 0:
            acc_ref[...] = term
        else:
            acc_ref[...] += term
    out_ref[...] = acc_ref[...].astype(BF16).reshape(out_ref.shape)


def whole_pairs(
    amplitudes, integrals, hh_coupling, thc_factor, thc_core, occ_energy, vir_energy, pair_owner
):
    row_count, col_count = lax.axis_size("row"), lax.axis_size("col")
    row, col = lax.axis_index("row"), lax.axis_index("col")
    devices = row_count * col_count
    virtual = vir_energy.shape[0]
    width = amplitudes.shape[1]
    orbs = width // virtual
    pairs_all = pair_owner.shape[0]
    mine = pairs_all // devices
    occupied_pairs = amplitudes.shape[0]
    points = thc_factor.shape[1] * devices
    block = points // row_count

    xt = thc_factor.T
    own = jnp.concatenate([xt[:, : virtual // 2], xt[:, virtual // 2 :], thc_core.astype(BF16)], 0)

    with jax.named_scope("hh_gather"):
        hh_parts = [hh_coupling] + [exchange(hh_coupling, t, 0) for t in range(1, row_count)]
    hh_rows = hh_coupling.shape[0]
    hh_all = jnp.zeros((hh_rows * row_count, occupied_pairs), BF16)
    for t, part in enumerate(hh_parts):
        hh_all = lax.dynamic_update_slice_in_dim(hh_all, part, (row ^ t) * hh_rows, 0)

    with jax.named_scope("z_gather"):
        z_flips = list(range(0, col_count, 2))
        stack = jnp.stack([own] + [exchange(own, 0, f) for f in z_flips[1:]])
    near = {0: stack}
    with jax.named_scope("xy_gather"):
        near[1] = exchange(stack, 1, 0)
        near[2] = exchange(stack, 2, 0)
        cut = len(z_flips) // 2
        low = exchange(near[1][:cut], 2, 0)
        high = exchange(near[2][cut:], 1, 0)
    arrays, places = [], []
    for t in (0, 1, 2):
        arrays.append(near[t])
        places.append([(t, f) for f in z_flips])
    arrays += [low, high]
    places += [[(3, f) for f in z_flips[:cut]], [(3, f) for f in z_flips[cut:]]]
    with jax.named_scope("core_gather"):
        for array, place in list(zip(arrays, places)):
            arrays.append(exchange(array, 0, 1))
            places.append([(r, f ^ 1) for r, f in place])

    owned = amplitudes[pair_owner]
    with jax.named_scope("pair_out"):
        outgoing = owned.reshape(devices, mine, orbs, virtual)
        arrived = lax.all_to_all(outgoing, AXES, split_axis=0, concat_axis=0, tiled=True)

    with jax.named_scope("coupled"):
        coupled = jnp.dot(hh_all, amplitudes, preferred_element_type=F32)

    xt_full, x_full, core_full = pl.pallas_call(
        functools.partial(place_kernel, (places, points, virtual)),
        out_shape=[
            jax.ShapeDtypeStruct((points, virtual), BF16),
            jax.ShapeDtypeStruct((virtual, points), BF16),
            jax.ShapeDtypeStruct((row_count, points, block), BF16),
        ],
        cost_estimate=pl.CostEstimate(flops=0, bytes_accessed=8 << 20, transcendentals=0),
        name="place",
    )(*arrays)

    ladder = pl.pallas_call(
        ladder_kernel,
        grid=(mine,),
        in_specs=[
            pl.BlockSpec((devices, pl.squeezed, orbs, virtual), lambda p: (0, p, 0, 0)),
            pl.BlockSpec((points, virtual), lambda p: (0, 0)),
            pl.BlockSpec((virtual, points), lambda p: (0, 0)),
            pl.BlockSpec((row_count, points, block), lambda p: (0, 0, 0)),
        ],
        out_specs=pl.BlockSpec((devices, pl.squeezed, orbs, virtual), lambda p: (0, p, 0, 0)),
        out_shape=jax.ShapeDtypeStruct((devices, mine, orbs, virtual), BF16),
        scratch_shapes=[pltpu.VMEM((virtual, virtual), F32)],
        cost_estimate=pl.CostEstimate(
            flops=mine * 2 * virtual * points * (2 * virtual + 2 * points),
            bytes_accessed=6 << 20,
            transcendentals=0,
        ),
        name="ladder",
    )(arrived, xt_full, x_full, core_full)

    with jax.named_scope("pair_back"):
        returned = lax.all_to_all(ladder, AXES, split_axis=0, concat_axis=0, tiled=True)
        returned = returned.reshape(pairs_all, width)

    coupled = lax.optimization_barrier(coupled)
    device = row * col_count + col
    vir_mine = lax.dynamic_slice_in_dim(vir_energy, device * orbs, orbs, 0)
    occ = owner_terms(pair_owner, occ_energy)
    vir_pairs = (vir_mine[:, None] + vir_energy[None, :]).reshape(1, width)
    denom = vir_pairs - occ[:, None]
    rest = integrals.astype(F32) + coupled + returned.astype(F32)
    update = 0.4 * owned.astype(F32) + 0.6 * rest / denom
    return update.astype(BF16)


def shared_pairs(
    amplitudes, integrals, hh_coupling, thc_factor, thc_core, occ_energy, vir_energy, pair_owner
):
    row_count, col_count = lax.axis_size("row"), lax.axis_size("col")
    row_index, col_index = lax.axis_index("row"), lax.axis_index("col")
    virtual = vir_energy.shape[0]
    column_width = amplitudes.shape[1]
    orb_block = column_width // virtual
    pairs_all = pair_owner.shape[0]
    pairs_col = pairs_all // col_count
    factor = lax.all_gather(thc_factor, AXES, axis=1, tiled=True)
    points = factor.shape[1]
    block_points = points // row_count
    core_block = lax.all_gather(thc_core, "col", axis=0, tiled=True)
    factor_block = lax.dynamic_slice_in_dim(factor, row_index * block_points, block_points, 1)
    owned = amplitudes[pair_owner]
    coupled = jnp.dot(
        lax.all_gather(hh_coupling, "row", axis=0, tiled=True),
        amplitudes,
        preferred_element_type=F32,
    )
    outgoing = owned.reshape(col_count, pairs_col, column_width)
    arrived = lax.all_to_all(outgoing, "col", split_axis=0, concat_axis=2, tiled=True)
    complete = lax.all_gather(arrived, "row", axis=2, tiled=True)
    complete = complete.reshape(pairs_col, virtual, virtual)
    half = jnp.einsum("pcd,dq->pcq", complete, factor_block, preferred_element_type=F32)
    half = half.astype(BF16)
    middle = jnp.einsum("cP,pcq->pPq", factor, half, preferred_element_type=F32)
    weighted = (core_block[None] * middle).astype(BF16)
    back = jnp.einsum("aP,pPq->paq", factor, weighted, preferred_element_type=F32).astype(BF16)
    vir_slice = virtual // row_count
    sectioned_back = back.reshape(pairs_col, row_count, vir_slice, block_points)
    gathered_back = lax.all_to_all(sectioned_back, "row", split_axis=1, concat_axis=3, tiled=True)
    gathered_back = gathered_back.reshape(pairs_col, vir_slice, row_count, block_points)
    factor_split = factor.reshape(virtual, row_count, block_points)
    partial_value = jnp.einsum(
        "parq,brq->rapb", gathered_back, factor_split, preferred_element_type=F32
    ).astype(BF16)
    ladder = jnp.sum(partial_value.astype(F32), axis=0).astype(BF16)
    ladder = ladder.reshape(col_count, orb_block, pairs_col, virtual)
    returned = lax.all_to_all(ladder, "col", split_axis=0, concat_axis=2, tiled=True)
    returned = (
        returned.reshape(orb_block, pairs_all, virtual)
        .transpose(1, 0, 2)
        .reshape(pairs_all, column_width)
    )
    device = row_index * col_count + col_index
    vir_mine = lax.dynamic_slice_in_dim(vir_energy, device * orb_block, orb_block, 0)
    occ = owner_terms(pair_owner, occ_energy)
    vir_pairs = (vir_mine[:, None] + vir_energy[None, :]).reshape(1, column_width)
    denom = vir_pairs - occ[:, None]
    rest = integrals.astype(F32) + coupled + returned.astype(F32)
    update = 0.4 * owned.astype(F32) + 0.6 * rest / denom
    return update.astype(BF16)


def per_device(*arguments):
    rows, cols = lax.axis_size("row"), lax.axis_size("col")
    pairs_all = arguments[-1].shape[0]
    if rows == 4 and cols & (cols - 1) == 0 and pairs_all % (rows * cols) == 0:
        return whole_pairs(*arguments)
    return shared_pairs(*arguments)


def solution(mesh):
    return jax.shard_map(
        per_device,
        mesh=mesh,
        in_specs=(
            P(None, ("row", "col")),
            P(None, ("row", "col")),
            P("row", None),
            P(None, ("row", "col")),
            P("col", "row"),
            P(),
            P(),
            P(),
        ),
        out_specs=P(None, ("row", "col")),
        check_vma=False,
    )
```
